256 devices in a mesh: req: 32 (over y, x, core), mlp: 8 (over z).
Axes of the slice: x: 4, y: 4, z: 8, core: 2. Of those that a mesh axis runs over, the one named last changes fastest.
Arguments:
- layer_input: bfloat16 [8192, 4096], P(('req', 'mlp')), may hold values from -6 to 6
- request_lengths: int32 [32, 4], P('req'), may hold values from 1 to 160, 256 in all within a row
- request_adapter: int32 [32, 4], P('req'), may hold values from 0 to 63, as said below
- slot_adapter_index: int32 [8], replicated, may hold values from 0 to 63, as said below
- query_weight: bfloat16 [4096, 2048], P(None, 'mlp'), may hold values from -0.09375 to 0.09375
- key_weight: bfloat16 [4096, 2048], P(None, 'mlp'), may hold values from -0.09375 to 0.09375
- value_weight: bfloat16 [4096, 2048], P(None, 'mlp'), may hold values from -0.09375 to 0.09375
- output_weight: bfloat16 [2048, 4096], P('mlp'), may hold values from -0.125 to 0.125
- query_norm_gain: float32 [2048], P('mlp'), may hold values from 0.1 to 1.9
- key_norm_gain: float32 [2048], P('mlp'), may hold values from 0.1 to 1.9
- query_down_factors: bfloat16 [4096, 128], replicated, may hold values from -0.09375 to 0.09375
- value_down_factors: bfloat16 [4096, 128], replicated, may hold values from -0.09375 to 0.09375
- query_up_factors: bfloat16 [128, 2048], P(None, 'mlp'), may hold values from -1.5 to 1.5
- value_up_factors: bfloat16 [128, 2048], P(None, 'mlp'), may hold values from -1.5 to 1.5
- attention_norm_gain: float32 [4096], replicated, may hold values from 0.1 to 1.9
- feedforward_norm_gain: float32 [4096], replicated, may hold values from 0.1 to 1.9
- gate_weight: bfloat16 [4096, 6144], P(None, ('req', 'mlp')), may hold values from -0.09375 to 0.09375
- up_weight: bfloat16 [4096, 6144], P(None, ('req', 'mlp')), may hold values from -0.09375 to 0.09375
- down_weight_transposed: bfloat16 [4096, 6144], P(None, ('req', 'mlp')), may hold values from -0.078125 to 0.078125
Outputs:
- layer_out: bfloat16 [8192, 4096], P(('req', 'mlp'))
The draws below stay inside these ranges and needn't reach their ends.
Inputs may be any that keep to these rules, and one draw needn't show every extreme that they name: `request_lengths`: the lengths of a group's requests sum to 256, and the longest request of every group has exactly 160 tokens. `slot_adapter_index`: 8 distinct adapter numbers. `request_adapter`: every request's adapter is one of the numbers in slot_adapter_index.
All inputs are finite; a program needn't handle non-finite values.
Results may differ from the reference program's by a relative error of at most 0.024.
Values may be sent and summed in bfloat16 or wider, within the bound.
A program may use at most 128 MiB of HBM per device.

```python
import math
import jax
import jax.numpy as jnp
import numpy as np
from jax import lax

MODEL_WIDTH = 4096
HEAD_SIZE = 128
LOCAL_HEADS = 16
FF = 6144
ADAPTER_RANK = 16
ADAPTERS = 64
ADAPTER_SLOTS = 8
REQ_G = 4
SINKS = 4
TOK_GROUP = 256
TOKENS = 8192
GROUPS = 32
LONGEST = 160
WINDOW = 96


def choose_adapters(key):
    others = jax.random.permutation(jax.random.fold_in(key, 101), ADAPTERS - 1)[:ADAPTER_SLOTS - 1].astype(jnp.int32)
    loaded = jnp.concatenate([others, jnp.full((1,), ADAPTERS - 1, jnp.int32)])
    arrangement = jax.random.permutation(jax.random.fold_in(key, 202), ADAPTER_SLOTS)
    loaded = loaded[arrangement]
    chosen_slots = jax.random.randint(jax.random.fold_in(key, 303), (GROUPS, REQ_G), 0, ADAPTER_SLOTS)
    return (loaded, loaded[chosen_slots])


def draw_slot_adapter_index(key, part):
    return choose_adapters(key)[0]


def draw_request_adapter(key, part):
    return choose_adapters(key)[1]


def levels(own_key, dims, split, low, top_value):
    def one(axis_at, blocks):
        draws = jax.random.uniform(jax.random.fold_in(jax.random.fold_in(own_key, 6), axis_at), (blocks,), jnp.float32, low / len(split), top_value / len(split))
        return jnp.repeat(jnp.exp(draws), dims[axis_at] // blocks).reshape((-1,) + (1,) * (len(dims) - axis_at - 1))

    level = one(*split[0])
    for cut in split[1:]:
        level = level * one(*cut)
    return level


def length_profile(number_of, total, bound, slope):
    portions = [(1 << 20) // math.isqrt(rank ** slope) + 1 for rank in range(2, number_of + 1)]
    spare, given = total - bound - (number_of - 1), [1] * (number_of - 1)
    while spare > 0:
        movable = [i for i in range(number_of - 1) if given[i] < bound]
        pool, left = sum([portions[i] for i in movable]), spare
        for i in movable:
            extra = min(bound - given[i], max(1, left * portions[i] // pool), spare)
            given[i] = given[i] + extra
            spare = spare - extra
    return np.array([bound] + given)


def ragged_sizes(rng, count, total, limit, skew):
    if count == 2:
        one = jax.random.randint(rng, (), max(1, total - limit), min(limit, total - 1) + 1)
        return jnp.stack([one, total - one])
    sizes = jnp.asarray(length_profile(count, total, limit, skew), jnp.int32)
    twos = (count - 1) // 2
    donor, taker = sizes[1:1 + 2 * twos:2], sizes[2:2 + 2 * twos:2]
    slack = jnp.minimum(donor - 1, limit - taker)
    moved = jax.random.randint(jax.random.fold_in(rng, 1), (twos,), 0, 1 << 20) % (slack + 1)
    sizes = sizes.at[1:1 + 2 * twos:2].set(donor - moved).at[2:2 + 2 * twos:2].set(taker + moved)
    return sizes[jax.random.permutation(jax.random.fold_in(rng, 2), count)]


def bell_draw(own_key, shape, spread, limit, shards=(), kind=jnp.bfloat16):
    loudness = levels(own_key, shape, shards, -0.22, 0.18) if shards else 1.0
    drawn = jax.random.normal(own_key, shape, jnp.float32) * spread * loudness
    return jnp.minimum(jnp.maximum(drawn, -limit), limit).astype(kind)


def setup_inputs(seed: int = 0) -> dict:
    key_of = jax.random.split(jax.random.key(seed), 20)
    layer_input = bell_draw(key_of[0], (TOKENS, MODEL_WIDTH), 1.0, 6.0, ((0, 256),))
    request_lengths = jax.vmap(lambda own: ragged_sizes(own, REQ_G, TOK_GROUP, LONGEST, 2))(jax.random.split(key_of[1], GROUPS)).reshape((GROUPS, REQ_G)).astype(jnp.int32)
    request_adapter = draw_request_adapter(jax.random.fold_in(key_of[19], 71), 0)
    slot_adapter_index = draw_slot_adapter_index(jax.random.fold_in(key_of[19], 71), 0)
    query_weight = bell_draw(key_of[4], (MODEL_WIDTH, LOCAL_HEADS * HEAD_SIZE), MODEL_WIDTH ** -0.5, 0.09375, ((1, 8),))
    key_weight = bell_draw(key_of[5], (MODEL_WIDTH, LOCAL_HEADS * HEAD_SIZE), MODEL_WIDTH ** -0.5, 0.09375, ((1, 8),))
    value_weight = bell_draw(key_of[6], (MODEL_WIDTH, LOCAL_HEADS * HEAD_SIZE), MODEL_WIDTH ** -0.5, 0.09375, ((1, 8),))
    output_weight = bell_draw(key_of[7], (LOCAL_HEADS * HEAD_SIZE, MODEL_WIDTH), (LOCAL_HEADS * HEAD_SIZE) ** -0.5, 0.125, ((0, 8),))
    query_norm_gain = jnp.clip(1.0 + 0.18 * jax.random.normal(key_of[8], (LOCAL_HEADS * HEAD_SIZE,), jnp.float32), 0.1, 1.9)
    key_norm_gain = jnp.clip(1.0 + 0.18 * jax.random.normal(key_of[9], (LOCAL_HEADS * HEAD_SIZE,), jnp.float32), 0.1, 1.9)
    query_down_factors = bell_draw(key_of[10], (MODEL_WIDTH, ADAPTER_SLOTS * ADAPTER_RANK), MODEL_WIDTH ** -0.5, 0.09375)
    value_down_factors = bell_draw(key_of[11], (MODEL_WIDTH, ADAPTER_SLOTS * ADAPTER_RANK), MODEL_WIDTH ** -0.5, 0.09375)
    query_up_factors = bell_draw(key_of[12], (ADAPTER_SLOTS * ADAPTER_RANK, LOCAL_HEADS * HEAD_SIZE), ADAPTER_RANK ** -0.5, 1.5, ((1, 8),))
    value_up_factors = bell_draw(key_of[13], (ADAPTER_SLOTS * ADAPTER_RANK, LOCAL_HEADS * HEAD_SIZE), ADAPTER_RANK ** -0.5, 1.5, ((1, 8),))
    attention_norm_gain = jnp.clip(1.0 + 0.18 * jax.random.normal(key_of[14], (MODEL_WIDTH,), jnp.float32), 0.1, 1.9)
    feedforward_norm_gain = jnp.clip(1.0 + 0.18 * jax.random.normal(key_of[15], (MODEL_WIDTH,), jnp.float32), 0.1, 1.9)
    gate_weight = bell_draw(key_of[16], (MODEL_WIDTH, FF), MODEL_WIDTH ** -0.5, 0.09375, ((1, 256),))
    up_weight = bell_draw(key_of[17], (MODEL_WIDTH, FF), MODEL_WIDTH ** -0.5, 0.09375, ((1, 256),))
    down_weight_transposed = bell_draw(key_of[18], (MODEL_WIDTH, FF), FF ** -0.5, 0.078125, ((1, 256),))
    return {"layer_input": layer_input, "request_lengths": request_lengths, "request_adapter": request_adapter, "slot_adapter_index": slot_adapter_index, "query_weight": query_weight, "key_weight": key_weight, "value_weight": value_weight, "output_weight": output_weight, "query_norm_gain": query_norm_gain, "key_norm_gain": key_norm_gain, "query_down_factors": query_down_factors, "value_down_factors": value_down_factors, "query_up_factors": query_up_factors, "value_up_factors": value_up_factors, "attention_norm_gain": attention_norm_gain, "feedforward_norm_gain": feedforward_norm_gain, "gate_weight": gate_weight, "up_weight": up_weight, "down_weight_transposed": down_weight_transposed}


epsilon = 1e-06
adapter_scale = 0.5
rope_theta = 500000.0

def rms_scale(inputs):
    return inputs * lax.rsqrt(lax.optimization_barrier(jnp.mean(inputs * inputs, axis=-1, keepdims=True)) + epsilon)

def rotary(inputs, position):
    half_dim = inputs.shape[-1] // 2
    exponent = jnp.arange(half_dim, dtype=jnp.float32) * (2.0 / inputs.shape[-1])
    frequency = rope_theta ** (-exponent)
    angles = position.astype(jnp.float32)[:, None] * frequency[None, :]
    cosine = jnp.cos(angles)[:, None, :]
    sine_part = jnp.sin(angles)[:, None, :]
    first_half = inputs[..., :half_dim]
    second = inputs[..., half_dim:]
    return jnp.concatenate([first_half * cosine - second * sine_part, second * cosine + first_half * sine_part], axis=-1)

def layout(lengths, adapters, slot_adapter_index, row_count):
    req_ends = jnp.cumsum(lengths).astype(jnp.int32)
    starts = req_ends - lengths
    places = jnp.arange(row_count, dtype=jnp.int32)
    member = ((places[:, None] >= starts[None, :]) & (places[:, None] < req_ends[None, :])).astype(jnp.int32)
    request = lax.optimization_barrier(jnp.sum(member * jnp.arange(lengths.shape[0], dtype=jnp.int32)[None, :], axis=1))
    position = places - lax.optimization_barrier(jnp.sum(member * starts[None, :], axis=1))
    chosen = lax.optimization_barrier(jnp.sum(member * adapters[None, :], axis=1))
    slot_ids = jnp.arange(slot_adapter_index.shape[0], dtype=jnp.int32)
    token_slot = lax.optimization_barrier(jnp.sum((chosen[:, None] == slot_adapter_index[None, :]).astype(jnp.int32) * slot_ids[None, :], axis=1))
    return (request, position, token_slot)

def attention(queries, key_heads, value_heads, request, position):
    scores = jnp.einsum('qhd,khd->hqk', queries.astype(jnp.float32), key_heads.astype(jnp.float32)) * HEAD_SIZE ** (-0.5)
    distance = position[:, None] - position[None, :]
    allowed = (request[:, None] == request[None, :]) & (distance >= 0) & ((distance < WINDOW) | (position[None, :] < SINKS))
    scores = jnp.where(allowed[None, :, :], scores, -1e+30)
    row_peak = lax.optimization_barrier(jnp.max(scores, axis=-1, keepdims=True))
    weights = jnp.exp(scores - row_peak)
    weights = (weights / lax.optimization_barrier(jnp.sum(weights, axis=-1, keepdims=True))).astype(jnp.bfloat16)
    context = jnp.einsum('hqk,khd->qhd', weights.astype(jnp.float32), value_heads.astype(jnp.float32))
    return context.astype(jnp.bfloat16)

def reference(layer_input, request_lengths, request_adapter, slot_adapter_index, query_weight, key_weight, value_weight, output_weight, query_norm_gain, key_norm_gain, query_down_factors, value_down_factors, query_up_factors, value_up_factors, attention_norm_gain, feedforward_norm_gain, gate_weight, up_weight, down_weight_transposed):

    def one_group(group_items):
        group_token_rows, lengths, adapters = group_items
        request, position, token_slot = layout(lengths, adapters, slot_adapter_index, TOK_GROUP)
        columns = jnp.arange(ADAPTER_SLOTS * ADAPTER_RANK, dtype=jnp.int32) // ADAPTER_RANK
        slot_match_mask = (columns[None, :] == token_slot[:, None]).astype(jnp.bfloat16)
        query_reduced = jnp.dot(group_token_rows, query_down_factors, preferred_element_type=jnp.float32).astype(jnp.bfloat16) * slot_match_mask
        value_reduced = jnp.dot(group_token_rows, value_down_factors, preferred_element_type=jnp.float32).astype(jnp.bfloat16) * slot_match_mask
        query_before_norm = jnp.dot(group_token_rows, query_weight, preferred_element_type=jnp.float32) + adapter_scale * jnp.dot(query_reduced, query_up_factors, preferred_element_type=jnp.float32)
        key_pre = jnp.dot(group_token_rows, key_weight, preferred_element_type=jnp.float32)
        value_before_adapter = jnp.dot(group_token_rows, value_weight, preferred_element_type=jnp.float32) + adapter_scale * jnp.dot(value_reduced, value_up_factors, preferred_element_type=jnp.float32)
        queries = rotary(rms_scale(query_before_norm.reshape(TOK_GROUP, LOCAL_HEADS, HEAD_SIZE)) * query_norm_gain.reshape(LOCAL_HEADS, HEAD_SIZE), position).astype(jnp.bfloat16)
        key_heads = rotary(rms_scale(key_pre.reshape(TOK_GROUP, LOCAL_HEADS, HEAD_SIZE)) * key_norm_gain.reshape(LOCAL_HEADS, HEAD_SIZE), position).astype(jnp.bfloat16)
        value_heads = value_before_adapter.astype(jnp.bfloat16).reshape(TOK_GROUP, LOCAL_HEADS, HEAD_SIZE)
        context = attention(queries, key_heads, value_heads, request, position).reshape(TOK_GROUP, LOCAL_HEADS * HEAD_SIZE)
        attn_out = jnp.dot(context, output_weight, preferred_element_type=jnp.float32)
        residual_mid = (group_token_rows.astype(jnp.float32) + rms_scale(attn_out) * attention_norm_gain).astype(jnp.bfloat16)
        gate_act = jnp.dot(residual_mid, gate_weight, preferred_element_type=jnp.float32)
        up_act = jnp.dot(residual_mid, up_weight, preferred_element_type=jnp.float32)
        hidden_act = (jax.nn.silu(gate_act) * up_act).astype(jnp.bfloat16)
        mlp_out = jnp.dot(hidden_act, down_weight_transposed.T, preferred_element_type=jnp.float32)
        return (residual_mid.astype(jnp.float32) + rms_scale(mlp_out) * feedforward_norm_gain).astype(jnp.bfloat16)
    grouped = layer_input.reshape(GROUPS, TOK_GROUP, MODEL_WIDTH)
    results = lax.map(one_group, (grouped, request_lengths, request_adapter))
    return results.reshape(TOKENS, MODEL_WIDTH)
```

```python
import functools

import jax
import jax.numpy as jnp
from jax import lax
from jax.experimental import pallas as pl
from jax.experimental.pallas import tpu as pltpu
from jax.sharding import PartitionSpec as P

HEAD = 128
RANK = 16
SINKS = 4
EPS = 1e-06
SCALE = 0.5
THETA = 500000.0
MESH = pl.DeviceIdType.MESH
f32 = jnp.float32
bf16 = jnp.bfloat16

NX, NY, NZ = 4, 4, 8
NR = NX * NY * 2
OFFS = (0, -1, 1, 2)


def dot(a, b):
    return jnp.dot(a, b, preferred_element_type=f32)


def dot_t(a, b):
    return lax.dot_general(a, b, (((1,), (1,)), ((), ())), preferred_element_type=f32)


def kernel(
    dims,
    lens_ref, adapt_ref, slots_ref,
    x_ref, wq_ref, wk_ref, wv_ref, wo_ref, qd_ref, vd_ref, gate_ref, up_ref, down_ref,
    qg_ref, kg_ref, qu_ref, vu_ref, ag_ref, fg_ref, freq_ref,
    out_ref,
    W, WO, XA, CA, AA, RM, WQ, LD, ACC, HID, PART, RB, MO, QB, KB, VB,
    lc, wos, wor, w1s, w1r, w2s, w2r, wss, wsr, xs, xr, cs, cr, as_, ar, p1s, p1r, p2s, p2r, p3s, p3r, sbs, sbr, rss, rsr,
):
    rows, width, ffd, win = dims
    toks = rows * NZ
    ow = width // NZ
    orow = 2 * HEAD // NR
    half = width // 2
    me = lax.axis_index("req")
    z = lax.axis_index("mlp")
    core = me % 2
    cx = (me // 2) % NX
    cy = me // (2 * NX)

    def rid(dx, dy, c):
        return ((cy + dy + NY) % NY) * (2 * NX) + ((cx + dx + NX) % NX) * 2 + c

    def zid(dz):
        return (z + dz + NZ) % NZ

    def copy(src, dst, ssem, rsem, dev):
        return pltpu.make_async_remote_copy(
            src_ref=src, dst_ref=dst, send_sem=ssem, recv_sem=rsem,
            device_id=dev, device_id_type=MESH,
        )

    def local(src, dst, i):
        return pltpu.make_async_copy(src, dst, lc.at[i])

    zpeers = [(me, zid(k)) for k in range(1, NZ)]
    xpeers = [(rid(k, 0, core), z) for k in (1, 2, 3)]
    ypeers = [(rid(0, k, core), z) for k in (1, 2, 3)]
    sib = (rid(0, 0, 1 - core), z)
    piece = core * (NX * NY) + cy * NX + cx
    up_z, dn_z = (me, zid(1)), (me, zid(-1))

    locs = [
        local(gate_ref, W.at[me, pl.ds(0, ffd), :], 0),
        local(up_ref, W.at[me, pl.ds(ffd, ffd), :], 1),
        local(down_ref, W.at[me, pl.ds(2 * ffd, ffd), :], 2),
        local(
            wo_ref.at[pl.ds(piece * orow, orow), pl.ds(z * ow, ow)],
            WO.at[core, cy, cx, :, pl.ds(z * ow, ow)], 3,
        ),
        local(x_ref, XA.at[pl.ds(z * rows, rows), :], 4),
        local(wq_ref, WQ.at[0], 5),
        local(wk_ref, WQ.at[1], 6),
        local(wv_ref, WQ.at[2], 7),
        local(qd_ref, LD.at[0], 8),
        local(vd_ref, LD.at[1], 9),
    ]
    for c in locs:
        c.start()

    barrier = pltpu.get_barrier_semaphore()
    peers = zpeers + xpeers + ypeers + [sib]
    for dev in peers:
        pl.semaphore_signal(barrier, inc=1, device_id=dev, device_id_type=MESH)
    pl.semaphore_wait(barrier, len(peers))

    def wo_send(k):
        t = zid(k)
        return copy(
            wo_ref.at[pl.ds(piece * orow, orow), pl.ds(t * ow, ow)],
            WO.at[core, cy, cx, :, pl.ds(z * ow, ow)],
            wos.at[k], wor.at[k], (me, t),
        )

    def wo_recv(k):
        t = zid(-k)
        return copy(
            wo_ref.at[pl.ds(piece * orow, orow), pl.ds(t * ow, ow)],
            WO.at[core, cy, cx, :, pl.ds(t * ow, ow)],
            wos.at[k], wor.at[k], (me, t),
        )

    for k in range(1, NZ):
        wo_send(k).start()

    def hops(d, s, c):
        return s <= 3 or c == d

    def ring(ref_of, ssem, rsem, first_of=None):
        def send(d, s, c):
            slot = zid(1 - s) if d == 0 else zid(s - 1)
            dst = ref_of(slot, c)
            src = first_of(c) if (s == 1 and first_of is not None) else dst
            return copy(src, dst, ssem.at[d, s - 1, c], rsem.at[d, s - 1, c], up_z if d == 0 else dn_z)

        def recv(d, s, c):
            slot = zid(-s) if d == 0 else zid(s)
            dst = ref_of(slot, c)
            return copy(dst, dst, ssem.at[d, s - 1, c], rsem.at[d, s - 1, c], up_z if d == 0 else dn_z)

        def first(c):
            for d in range(2):
                send(d, 1, c).start()

        def forward(s):
            for c in range(2):
                for d in range(2):
                    if hops(d, s, c):
                        recv(d, s, c).wait_recv()
                        if s < 4 and hops(d, s + 1, c):
                            send(d, s + 1, c).start()

        def drain():
            for s in range(1, 5):
                for c in range(2):
                    for d in range(2):
                        if hops(d, s, c):
                            send(d, s, c).wait_send()

        return first, forward, drain

    x_first, x_forward, x_drain = ring(
        lambda slot, c: XA.at[pl.ds(slot * rows, rows), pl.ds(c * half, half)], xs, xr,
        lambda c: x_ref.at[:, pl.ds(c * half, half)],
    )
    c_first, c_forward, c_drain = ring(lambda slot, c: CA.at[slot, c], cs, cr)
    a_first, a_forward, a_drain = ring(
        lambda slot, c: AA.at[slot, pl.ds(c * (toks // 2), toks // 2), :], as_, ar
    )
    x_first(0)
    x_first(1)

    def place(h, o, j, c):
        a, b = OFFS[o], OFFS[j]
        return rid(a, b, c) if h == 0 else rid(b, a, c)

    def block(r, h):
        return W.at[r, :, pl.ds(h * half, half)]

    def along1(h, d):
        return (rid(d, 0, core), z) if h == 0 else (rid(0, d, core), z)

    def along2(h, d):
        return (rid(0, d, core), z) if h == 0 else (rid(d, 0, core), z)

    def same(ref, ssem, rsem, dev):
        return copy(ref, ref, ssem, rsem, dev)

    def p1(h, k, o=0):
        return same(block(place(h, o, 0, core), h), p1s.at[h, k], p1r.at[h, k], along1(h, (1, -1, 2)[k]))

    def p2(h, o, d, j=0):
        return same(block(place(h, o, j, core), h), p2s.at[h, o, d], p2r.at[h, o, d], along2(h, (1, -1)[d]))

    def p3(h, o, j):
        d = 0 if o < 2 else 1
        return same(block(place(h, o, j, core), h), p3s.at[h, o], p3r.at[h, o], along2(h, (1, -1)[d]))

    def sb(h, o, j, c):
        return same(block(place(h, o, j, c), h), sbs.at[h, o, j], sbr.at[h, o, j], sib)

    def w1(h, k, o):
        a = (0, -1, 1, 2)[o]
        part = pl.ds(h * half, half)
        py, px = (cy, (cx + a + NX) % NX) if h == 0 else ((cy + a + NY) % NY, cx)
        return same(WO.at[core, py, px, :, part], w1s.at[h, k], w1r.at[h, k], along1(h, (1, -1, 2)[k]))

    def w2(h, k, o):
        a = (0, -1, 1, 2)[o]
        part = pl.ds(h * half, half)
        if h == 0:
            ref = WO.at[core, (cy + a + NY) % NY, :, :, part]
        else:
            ref = WO.at[core, :, (cx + a + NX) % NX, :, part]
        return same(ref, w2s.at[h, k], w2r.at[h, k], along2(h, (1, -1, 2)[k]))

    def wsib(c):
        return same(WO.at[c], wss.at[0], wsr.at[0], sib)

    for c in locs[:3]:
        c.wait()
    for h in range(2):
        for k in range(2):
            p1(h, k).start()
        sb(h, 0, 0, core).start()
    locs[3].wait()
    for k in range(1, NZ):
        wo_recv(k).wait_recv()
    for h in range(2):
        for k in range(3):
            w1(h, k, 0).start()
    for h in range(2):
        p1(h, 2).start()

    def w1_task():
        for h in range(2):
            for k in range(3):
                w1(h, k, k + 1).wait_recv()
            for k in range(3):
                w2(h, k, 0).start()
        for h in range(2):
            for d in range(2):
                p2(h, 0, d).start()

    def w2_task():
        for h in range(2):
            for k in range(3):
                w2(h, k, k + 1).wait_recv()
        wsib(core).start()

    def p1_task(k):
        for h in range(2):
            p1(h, k, k + 1).wait_recv()
            for d in range(2):
                p2(h, k + 1, d).start()
            sb(h, k + 1, 0, core).start()

    def p2_task(o):
        for h in range(2):
            for d in range(2):
                p2(h, o, d, d + 1).wait_recv()
                if d == (0 if o < 2 else 1):
                    p3(h, o, d + 1).start()
                sb(h, o, d + 1, core).start()

    def p3_task(o):
        for h in range(2):
            p3(h, o, 3).wait_recv()
            sb(h, o, 3, core).start()

    lens = [lens_ref[0, i] for i in range(4)]
    ends = [lens[0], lens[0] + lens[1], lens[0] + lens[1] + lens[2]]
    slot_of = []
    for i in range(4):
        found = jnp.int32(0)
        for s in range(8):
            found = found + jnp.where(adapt_ref[0, i] == slots_ref[s], s, 0)
        slot_of.append(found)
    tok = lax.broadcasted_iota(jnp.int32, (toks, HEAD), 0)
    start = jnp.zeros((toks, HEAD), jnp.int32)
    slot = jnp.zeros((toks, HEAD), jnp.int32) + slot_of[0]
    for i in range(3):
        later = tok >= ends[i]
        start = jnp.where(later, ends[i], start)
        slot = jnp.where(later, slot_of[i + 1], slot)
    lane = lax.broadcasted_iota(jnp.int32, (toks, HEAD), 1)
    slot_mask = jnp.where(lane // RANK == slot, 1.0, 0.0).astype(bf16)
    angle = (tok - start).astype(f32) * freq_ref[...]
    cosine = jnp.cos(angle)
    sine = jnp.sin(angle)
    sine = jnp.where(lane < HEAD // 2, -sine, sine)
    start_q = jnp.concatenate([start] * (toks // HEAD), axis=1)
    tq = lax.broadcasted_iota(jnp.int32, (toks, toks), 0)
    tk = lax.broadcasted_iota(jnp.int32, (toks, toks), 1)
    allowed = (tk >= start_q) & (tk <= tq) & ((tq - tk < win) | (tk - start_q < SINKS))

    x_forward(1)
    w1_task()
    x_forward(2)
    p1_task(0)
    p1_task(1)
    x_forward(3)
    p1_task(2)
    x_forward(4)
    for c in locs[4:]:
        c.wait()

    rowsx = XA[...]
    low_q = dot(rowsx, LD[0]).astype(bf16) * slot_mask
    q_pre = dot(rowsx, WQ[0]) + SCALE * dot(low_q, qu_ref[...])
    k_pre = dot(rowsx, WQ[1])
    low_v = dot(rowsx, LD[1]).astype(bf16) * slot_mask
    v_pre = dot(rowsx, WQ[2]) + SCALE * dot(low_v, vu_ref[...])

    def rotate(v, gain):
        v = v * lax.rsqrt(jnp.mean(v * v, axis=-1, keepdims=True) + EPS) * gain
        return (v * cosine + pltpu.roll(v, HEAD // 2, 1) * sine).astype(bf16)

    QB[...] = q_pre
    KB[...] = k_pre
    VB[...] = v_pre.astype(bf16)
    w2_task()
    p2_task(0)
    for h in range(2):
        cols = pl.ds(h * HEAD, HEAD)
        query = rotate(QB[:, cols], qg_ref[:, cols])
        key = rotate(KB[:, cols], kg_ref[:, cols])
        scores = jnp.where(allowed, dot_t(query, key) * HEAD ** (-0.5), -1e30)
        peak = jnp.max(scores, axis=-1, keepdims=True)
        weights = jnp.exp(scores - peak)
        weights = (weights / jnp.sum(weights, axis=-1, keepdims=True)).astype(bf16)
        CA[z, h] = dot(weights, VB[:, cols]).astype(bf16)
        c_first(h)

    c_forward(1)
    p2_task(1)
    c_forward(2)
    c_forward(3)
    c_forward(4)
    wsib(1 - core).wait_recv()

    def project(i, acc):
        w = WO[:, :, :, :, pl.ds(pl.multiple_of(i * ow, ow), ow)].reshape(2 * HEAD, ow)
        return acc + dot(jnp.concatenate([CA[i, 0], CA[i, 1]], axis=1), w)

    own = lax.fori_loop(0, NZ, project, jnp.zeros((toks, ow), f32))
    AA[z] = own.astype(bf16)
    a_first(0)
    a_first(1)
    p2_task(2)
    a_forward(1)
    p2_task(3)
    a_forward(2)
    p3_task(0)
    p3_task(1)
    a_forward(3)
    p3_task(2)
    p3_task(3)
    for o in range(4):
        for h in range(2):
            for j in range(4):
                sb(h, o, j, 1 - core).wait_recv()
    a_forward(4)

    def squares(i, acc):
        a = AA[i].astype(f32)
        return acc + jnp.sum(a * a, axis=-1, keepdims=True)

    total = lax.fori_loop(0, NZ, squares, jnp.zeros((toks, 1), f32))
    inv = lax.rsqrt(total * (1.0 / width) + EPS)
    ACC[...] = jnp.zeros_like(ACC)

    def gate_up(i, _):
        cols = pl.ds(pl.multiple_of(i * ow, ow), ow)
        res = (XA[:, cols].astype(f32) + AA[i].astype(f32) * inv * ag_ref[:, cols]).astype(bf16)
        RM[:, cols] = res
        for m in range(2):
            w = W[:, pl.ds(m * ffd, ffd), cols].reshape(NR * ffd, ow)
            ACC[m] += dot_t(res, w)
        return 0

    lax.fori_loop(0, NZ, gate_up, 0)
    g = ACC[0]
    HID[...] = (g / (1.0 + jnp.exp(-g)) * ACC[1]).astype(bf16)

    nch = PART.shape[0]
    cw = width // nch

    def rs_part(d, s):
        if s == 1:
            return pl.ds(d * (cw // 2), cw // 2)
        return pl.ds(0, cw)

    def rs_rows(d, s):
        return pl.ds((zid(5 - s) if d == 0 else zid(s - 5)) * rows, rows)

    def rs(d, s, j):
        if s == 1:
            src = PART.at[j, rs_rows(d, 1), rs_part(d, 1)]
        else:
            src = RB.at[d, s - 2, j]
        dst = RB.at[d, s - 1, j, :, rs_part(d, s)]
        return copy(src, dst, rss.at[d, s - 1, j], rsr.at[d, s - 1, j], up_z if d == 0 else dn_z)

    def down(j, _):
        w = W[:, pl.ds(2 * ffd, ffd), pl.ds(pl.multiple_of(j * cw, cw), cw)].reshape(NR * ffd, cw)
        PART[j] = dot(HID[...], w).astype(bf16)
        for d in range(2):
            rs(d, 1, j).start()
        return 0

    lax.fori_loop(0, nch, down, 0)
    for s in range(1, 4):

        def step(j, _, s=s):
            for d in range(2):
                rs(d, s, j).wait_recv()
                mine = PART[j, rs_rows(d, s + 1), :].astype(f32)
                if s == 1:
                    near, far = rs_part(d, 1), rs_part(1 - d, 1)
                    got = RB[d, 0, j, :, near].astype(f32)
                    lo = d * (cw // 2)
                    RB[d, 0, j, :, near] = (got + mine[:, lo:lo + cw // 2]).astype(bf16)
                    lo = (1 - d) * (cw // 2)
                    RB[d, 0, j, :, far] = mine[:, lo:lo + cw // 2].astype(bf16)
                else:
                    RB[d, s - 1, j] = (RB[d, s - 1, j].astype(f32) + mine).astype(bf16)
                rs(d, s + 1, j).start()
            return 0

        lax.fori_loop(0, nch, step, 0)

    def finish(j, acc):
        for d in range(2):
            rs(d, 4, j).wait_recv()
        v = (
            PART[j, pl.ds(z * rows, rows), :].astype(f32)
            + RB[0, 3, j].astype(f32)
            + RB[1, 3, j].astype(f32)
        )
        MO[:, pl.ds(pl.multiple_of(j * cw, cw), cw)] = v
        return acc + jnp.sum(v * v, axis=-1, keepdims=True)

    total2 = lax.fori_loop(0, nch, finish, jnp.zeros((rows, 1), f32))
    inv2 = lax.rsqrt(total2 * (1.0 / width) + EPS)
    out_ref[...] = (
        RM[pl.ds(z * rows, rows), :].astype(f32) + MO[...] * inv2 * fg_ref[...]
    ).astype(bf16)

    for k in range(1, NZ):
        wo_send(k).wait_send()
    wsib(core).wait_send()
    x_drain()
    c_drain()
    a_drain()
    for h in range(2):
        for k in range(3):
            p1(h, k).wait_send()
            w1(h, k, 0).wait_send()
            w2(h, k, 0).wait_send()
        for o in range(4):
            for d in range(2):
                p2(h, o, d).wait_send()
            p3(h, o, 1).wait_send()
            for j in range(4):
                sb(h, o, j, core).wait_send()

    def drain_rs(j, _):
        for d in range(2):
            for s in range(1, 5):
                rs(d, s, j).wait_send()
        return 0

    lax.fori_loop(0, nch, drain_rs, 0)


def shards(
    layer_input, request_lengths, request_adapter, slot_adapter_index,
    query_weight, key_weight, value_weight, output_weight,
    query_norm_gain, key_norm_gain, query_down_factors, value_down_factors,
    query_up_factors, value_up_factors, attention_norm_gain, feedforward_norm_gain,
    gate_weight, up_weight, down_weight_transposed,
):
    rows, width = layer_input.shape
    ffd = gate_weight.shape[1]
    toks = rows * NZ
    orow = 2 * HEAD // NR
    nch = 4
    lane = jnp.arange(HEAD, dtype=f32) % (HEAD // 2)
    freq = (THETA ** (-(lane * (2.0 / HEAD))))[None, :]
    any_ = pl.BlockSpec(memory_space=pl.ANY)
    smem = pl.BlockSpec(memory_space=pltpu.SMEM)
    vmem = pl.BlockSpec(memory_space=pltpu.VMEM)
    V = pltpu.VMEM
    D = pltpu.SemaphoreType.DMA
    scratch = [
        V((NR, 3 * ffd, width), bf16),
        V((2, NY, NX, orow, width), bf16),
        V((toks, width), bf16),
        V((NZ, 2, toks, HEAD), bf16),
        V((NZ, toks, width // NZ), bf16),
        V((toks, width), bf16),
        V((3, width, 2 * HEAD), bf16),
        V((2, width, HEAD), bf16),
        V((2, toks, NR * ffd), f32),
        V((toks, NR * ffd), bf16),
        V((nch, toks, width // nch), bf16),
        V((2, 4, nch, rows, width // nch), bf16),
        V((rows, width), f32),
        V((toks, 2 * HEAD), f32),
        V((toks, 2 * HEAD), f32),
        V((toks, 2 * HEAD), bf16),
        D((10,)), D((NZ,)), D((NZ,)),
        D((2, 3)), D((2, 3)), D((2, 3)), D((2, 3)), D((1,)), D((1,)),
        D((2, 4, 2)), D((2, 4, 2)), D((2, 4, 2)), D((2, 4, 2)), D((2, 4, 2)), D((2, 4, 2)),
        D((2, 3)), D((2, 3)), D((2, 4, 2)), D((2, 4, 2)), D((2, 4)), D((2, 4)),
        D((2, 4, 4)), D((2, 4, 4)), D((2, 4, nch)), D((2, 4, nch)),
    ]
    return pl.pallas_call(
        functools.partial(kernel, (rows, width, ffd, toks * 3 // 8)),
        out_shape=jax.ShapeDtypeStruct((rows, width), bf16),
        in_specs=[smem] * 3 + [any_] * 10 + [vmem] * 7,
        out_specs=vmem,
        scratch_shapes=scratch,
        compiler_params=pltpu.CompilerParams(
            collective_id=1, has_side_effects=True, vmem_limit_bytes=60 << 20
        ),
        name="layer",
    )(
        request_lengths, request_adapter, slot_adapter_index,
        layer_input, query_weight, key_weight, value_weight, output_weight,
        query_down_factors, value_down_factors,
        gate_weight.T, up_weight.T, down_weight_transposed.T,
        query_norm_gain[None, :], key_norm_gain[None, :], query_up_factors, value_up_factors,
        attention_norm_gain[None, :], feedforward_norm_gain[None, :], freq,
    )


def solution(mesh):
    return jax.shard_map(
        shards,
        mesh=mesh,
        in_specs=(
            P(("req", "mlp"), None), P("req", None), P("req", None), P(),
            P(None, "mlp"), P(None, "mlp"), P(None, "mlp"), P("mlp", None),
            P("mlp"), P("mlp"), P(), P(), P(None, "mlp"), P(None, "mlp"), P(), P(),
            P(None, ("req", "mlp")), P(None, ("req", "mlp")), P(None, ("req", "mlp")),
        ),
        out_specs=P(("req", "mlp"), None),
        check_vma=False,
    )
```
